32 devices in a mesh: gx: 8 (over z, y), gy: 4 (over x, core).
Axes of the slice: x: 2, y: 2, z: 4, core: 2. Of those that a mesh axis runs over, the one named last changes fastest.
Arguments:
- inputs: bfloat16 [16, 16, 48, 128], P('gx', 'gy'), may hold values from -6 to 6
- cotangent: bfloat16 [16, 16, 48, 128], P('gx', 'gy'), may hold values from -6 to 6
- kernel: bfloat16 [27, 128, 128], replicated, may hold values from -0.109375 to 0.109375
Outputs:
- input_grad: bfloat16 [16, 16, 48, 128], P('gx', 'gy')
- kernel_grad: float32 [27, 128, 128], P(None, 'gx', 'gy')
The draws below stay inside these ranges and needn't reach their ends.
All inputs are finite; a program needn't handle non-finite values.
Results may differ from the reference program's by a relative error of at most 0.0023.
Values may be sent and summed in bfloat16 or wider, within the bound.
No kernel may reach another device: no remote copies, remote signals or barrier semaphores. Data moves between devices by JAX's collectives and lax.ppermute only.
A program may use at most 64 MiB of HBM per device.

```python
import math
import jax
import jax.numpy as jnp
from jax import lax

C = 128
DEPTH = 48
NX = 16
NY = 16


def raised(values, own_key, source, target, blocks, factor):
    owner, partner = [(jnp.arange(values.shape[dim]) // (values.shape[dim] // blocks)).reshape([-1 if axis == dim else 1 for axis in range(values.ndim)]) for dim in (source, target)]
    chosen = jax.random.permutation(own_key, blocks)[partner]
    strong = (owner == chosen) | (owner == (partner + blocks // 2) % blocks)
    return jnp.where(strong, factor * values, values)


def shard_levels(key, dims, shards, smallest, top_value):
    def one(axis_at, parts):
        heights = jax.random.uniform(jax.random.fold_in(jax.random.fold_in(key, 6), axis_at), (parts,), jnp.float32, smallest / len(shards), top_value / len(shards))
        return jnp.repeat(jnp.exp(heights), dims[axis_at] // parts).reshape((-1,) + (1,) * (len(dims) - axis_at - 1))

    loudness = one(*shards[0])
    for cut in shards[1:]:
        loudness = loudness * one(*cut)
    return loudness


def centred(stream_key, shape, width, reach, shards=(), held_as=jnp.bfloat16):
    values = width * jax.random.normal(stream_key, shape, jnp.float32)
    if shards:
        values = values * shard_levels(stream_key, shape, shards, -0.22, 0.18)
    return jnp.clip(values, -reach, reach).astype(held_as)


def heavy_noise(key, shape, spread, reach, cuts, heavy, kind=jnp.bfloat16):
    result = spread * jax.random.normal(key, shape, jnp.float32)
    if cuts:
        result = result * shard_levels(key, shape, cuts, -0.22, 0.18)
    return jnp.clip(raised(result, jax.random.fold_in(key, 3), *heavy), -reach, reach).astype(kind)


def setup_inputs(seed: int = 0) -> dict:
    key_list = jax.random.split(jax.random.key(seed), 4)
    return {
        "inputs": heavy_noise(key_list[0], (NX, NY, DEPTH, C), 1.0, 6.0, ((0, 8), (1, 4)), (1, 3, 4, 2.0)),
        "cotangent": heavy_noise(key_list[1], (NX, NY, DEPTH, C), 1.0, 6.0, ((0, 8), (1, 4)), (0, 3, 8, 2.0)),
        "kernel": centred(key_list[2], (27, C, C), (27 * C) ** -0.5, 0.109375),
    }


def reference(inputs, cotangent, kernel):
    widthx, widthy, depth, chans = inputs.shape
    values = inputs.astype(jnp.float32)
    act = (values * 0.5 * (1.0 + lax.erf(values / math.sqrt(2.0)))).astype(jnp.bfloat16)
    slope = 0.5 * (1.0 + lax.erf(values / math.sqrt(2.0))) + values * jnp.exp(-0.5 * values * values) / math.sqrt(2.0 * math.pi)
    act_pad = jnp.pad(act, ((1, 1), (1, 1), (1, 1), (0, 0)))
    cot_pad = jnp.pad(cotangent, ((1, 1), (1, 1), (1, 1), (0, 0)))
    cot_flat = cotangent.reshape(-1, chans)
    back = jnp.zeros((widthx * widthy * depth, chans), jnp.float32)
    grads = []
    for jx in range(3):
        for jy in range(3):
            for jz in range(3):
                tap = jx * 9 + jy * 3 + jz
                apiece = act_pad[jx:jx + widthx, jy:jy + widthy, jz:jz + depth].reshape(-1, chans)
                grads.append(jnp.dot(apiece.T, cot_flat, preferred_element_type=jnp.float32))
                gpiece = cot_pad[2 - jx:2 - jx + widthx, 2 - jy:2 - jy + widthy, 2 - jz:2 - jz + depth].reshape(-1, chans)
                back = back + jnp.dot(gpiece, kernel[tap].T, preferred_element_type=jnp.float32)
    input_grad = (slope * back.reshape(widthx, widthy, depth, chans)).astype(jnp.bfloat16)
    kernel_grad = jnp.stack(grads) / math.sqrt(widthx * widthy * depth)
    return (input_grad, kernel_grad)
```

```python
import functools
import math

import jax
import jax.numpy as jnp
from jax import lax
from jax.experimental import pallas as pl
from jax.experimental.pallas import tpu as pltpu
from jax.sharding import PartitionSpec as P


AXES = ("gx", "gy")
BF16 = jnp.bfloat16
F32 = jnp.float32


def spot():
    at_x, at_y = lax.axis_index("gx"), lax.axis_index("gy")
    return at_x // 2, at_x % 2, at_y // 2, at_y % 2


def swap(array, size, mask):
    return lax.ppermute(array, AXES, [(i, i ^ mask) for i in range(size)])


def pairs_along(count, stride, size, odd):
    found = []
    for i in range(size):
        at = (i // stride) % count
        to = at ^ 1 if not odd else (at - 1 if at % 2 == 0 else at + 1)
        if 0 <= to < count:
            found.append((i, i + (to - at) * stride))
    return found


def call(body, outs, args, scratch=(), flops=0, moved=0):
    vmem = pl.BlockSpec(memory_space=pltpu.VMEM)
    return pl.pallas_call(
        body,
        out_shape=tuple(jax.ShapeDtypeStruct(s, d) for s, d in outs),
        in_specs=[vmem] * len(args),
        out_specs=tuple(vmem for _ in outs),
        scratch_shapes=list(scratch),
        cost_estimate=pl.CostEstimate(flops=flops, bytes_accessed=moved, transcendentals=0),
    )(*args)


def one_hot(source, rows):
    at = lax.broadcasted_iota(jnp.int32, (rows, source.shape[1]), 0)
    return (at == source).astype(F32).astype(BF16)


def pack_body(dims, act_ref, cot_ref, outer_ref, inner_ref, *outs):
    parts_x, parts_y, wx, wy, depth, chans = dims
    _, lo, chip, core = spot()
    chips = parts_y // 2
    block_i, half = chans // parts_x, chans // 2
    pair_o = 2 * (chans // parts_y)
    rows, edge = wx * wy * depth, wy * depth // 2
    both = jnp.concatenate(
        [act_ref[...].reshape(rows, chans), cot_ref[...].reshape(rows, chans)], axis=1
    )
    rim = outer_ref[...].reshape(2 * edge, chans)
    rim = jnp.concatenate([rim[:edge], rim[edge:]], axis=1)
    lane = lax.broadcasted_iota(jnp.int32, (1, chans), 1)
    place = 0
    for flip_lo in range(2):
        for flip in range(chips):
            to_lo, to_chip = lo ^ flip_lo, chip ^ flip
            group = jnp.right_shift(lane, block_i.bit_length() - 1)
            from_act = (2 * group + to_lo) * block_i + (lane & (block_i - 1))
            column = to_chip * pair_o + lane - half
            from_cot = jnp.where(lane < half + pair_o, chans + column, -1)
            body = one_hot(jnp.where(lane < half, from_act, from_cot), 2 * chans)
            first = to_chip * pair_o + lane
            second = jnp.where(lane < 2 * pair_o, chans + first - pair_o, -1)
            ends = one_hot(jnp.where(lane < pair_o, first, second), 2 * chans)
            outs[place][:rows] = jnp.dot(both, body, preferred_element_type=F32).astype(BF16)
            outs[place][rows:] = jnp.dot(rim, ends, preferred_element_type=F32).astype(BF16)
            place += 1
    for out, column in ((outs[place], (1 - core) * (wy - 1)), (outs[place + 1], core * (wy - 1))):
        for x in range(wx):
            out[(x + 1) * depth : (x + 2) * depth] = cot_ref[x, column]

        @pl.when(lo == 0)
        def _(out=out, column=column):
            out[:depth] = outer_ref[0, column]
            out[(wx + 1) * depth :] = inner_ref[0, column]

        @pl.when(lo == 1)
        def _(out=out, column=column):
            out[:depth] = inner_ref[0, column]
            out[(wx + 1) * depth :] = outer_ref[0, column]


def raw_body(dims, *refs):
    parts_x, parts_y, wx, wy, depth, chans = dims
    hi, lo, chip, core = spot()
    his, chips = parts_x // 2, parts_y // 2
    block_i, half = chans // parts_x, chans // 2
    block_o = chans // parts_y
    rows, edge = wx * wy * depth, wy * depth // 2
    blocks = refs[: 4 * chips]
    outs = refs[4 * chips : 4 * chips + his]
    acts, cots, wide, sums = refs[4 * chips + his :]
    total_y = wy * parts_y
    blank = jnp.zeros((depth, chans), BF16)
    for x in range(2 * wx + 2):
        for slot in range(3):
            cots[slot, x, 0] = blank
            cots[slot, x, total_y + 1] = blank
    lane = lax.broadcasted_iota(jnp.int32, (1, chans), 1)

    def place_cot(value, at, x, y):
        count = value.shape[0] // depth
        wide_value = value.astype(F32)
        for slot in range(3):
            shifts = [(slot * block_o - at - c * block_o) % chans for c in range(2)]
            moved = [pltpu.roll(wide_value, s, 1) if s else wide_value for s in shifts]
            picked = jnp.where(core == 0, moved[0], moved[1])
            keep = (lane >= slot * block_o) & (lane < (slot + 1) * block_o)
            picked = jnp.where(keep, picked, 0.0).astype(BF16)
            cots[slot, x, pl.ds(y, count)] = picked.reshape(count, depth, chans)

    place = 0
    for flip_core in range(2):
        for flip_lo in range(2):
            for flip in range(chips):
                block = blocks[place]
                place += 1
                from_lo = lo ^ flip_lo
                from_y = (2 * (chip ^ flip) + (core ^ flip_core)) * wy
                for x in range(wx):
                    part = block[x * wy * depth : (x + 1) * wy * depth]
                    acts[from_lo * wx + x, pl.ds(from_y, wy)] = part.reshape(wy, depth, chans)
                    place_cot(part, half, from_lo * wx + x + 1, from_y + 1)
                rim_x = from_lo * (2 * wx + 1)
                rim = block[rows:]
                place_cot(rim, 0, rim_x, from_y + 1)
                place_cot(rim, 2 * block_o, rim_x, from_y + 1 + wy // 2)
    plane = total_y * depth
    for x in range(2 * wx + 2):
        merged = cots[0, x, 2 : total_y + 2] + cots[1, x, 1 : total_y + 1] + cots[2, x, 0:total_y]
        wide[x * plane : (x + 1) * plane] = merged.reshape(plane, chans)
    z = lax.broadcasted_iota(jnp.int32, (depth, 1), 0)
    sums[...] = jnp.zeros_like(sums)
    for x in range(2 * wx):
        flat = acts[x].reshape(plane, chans)
        middle = flat[:, :half].astype(F32).reshape(total_y, depth, half)
        below = jnp.where(z > 0, pltpu.roll(middle, 1, 1), 0.0)
        above = jnp.where(z < depth - 1, pltpu.roll(middle, depth - 1, 1), 0.0)
        left = jnp.concatenate([below, middle, above], axis=2).reshape(plane, 3 * half)
        right = jnp.concatenate(
            [wide[(x + 2 - jx) * plane : (x + 3 - jx) * plane] for jx in range(3)], axis=1
        )
        sums[...] += lax.dot_general(
            left.astype(BF16), right, (((0,), (0,)), ((), ())), preferred_element_type=F32
        )
    for flip, out in enumerate(outs):
        start = pl.multiple_of((hi ^ flip) * block_i, block_i)
        for jx in range(3):
            for jz in range(3):
                out[(3 * jx + jz) * block_i : (3 * jx + jz + 1) * block_i] = sums[
                    pl.ds(jz * half + start, block_i), jx * chans : (jx + 1) * chans
                ]


def back_body(dims, inputs_ref, cot_ref, outer_ref, inner_ref, even_ref, odd_ref, kernel_ref, out_ref, pad):
    _, _, wx, wy, depth, chans = dims
    _, lo, _, core = spot()
    rows = wx * wy * depth
    pad[1 : wx + 1, 1 : wy + 1] = cot_ref[...]
    pad[(1 - lo) * (wx + 1), 1 : wy + 1] = inner_ref[0]
    pad[lo * (wx + 1), 1 : wy + 1] = outer_ref[0]
    even, odd = (1 - core) * (wy + 1), core * (wy + 1)
    for x in range(wx + 2):
        pad[x, even] = even_ref[x * depth : (x + 1) * depth]
        pad[x, odd] = odd_ref[x * depth : (x + 1) * depth]
    left, right = [], []
    for jx in range(3):
        for jy in range(3):
            first = jx * 9 + jy * 3
            piece = pad[2 - jx : 2 - jx + wx, 2 - jy : 2 - jy + wy]
            left.append(piece.reshape(rows, chans))
            right.append(kernel_ref[first : first + 3].reshape(3 * chans, chans))
    product = lax.dot_general(
        jnp.concatenate(left, axis=1),
        jnp.concatenate(right, axis=1),
        (((1,), (1,)), ((), ())),
        preferred_element_type=F32,
    ).reshape(wx * wy, depth, 3 * chans)
    z = lax.broadcasted_iota(jnp.int32, (depth, 1), 0)
    low = product[:, :, :chans]
    high = product[:, :, 2 * chans :]
    back = product[:, :, chans : 2 * chans]
    back += jnp.where(z < depth - 1, pltpu.roll(low, depth - 1, 1), 0.0)
    back += jnp.where(z > 0, pltpu.roll(high, 1, 1), 0.0)
    values = inputs_ref[...].astype(F32).reshape(wx * wy, depth, chans)
    cdf = 0.5 * (1.0 + lax.erf(values / math.sqrt(2.0)))
    slope = cdf + values * jnp.exp(-0.5 * values * values) / math.sqrt(2.0 * math.pi)
    out_ref[...] = (slope * back).astype(BF16).reshape(wx, wy, depth, chans)


def final_body(dims, voxels, *refs):
    parts_x, parts_y, _, _, _, chans = dims
    block_i, block_o = chans // parts_x, chans // parts_y
    out = refs[-1]
    total = refs[0][...]
    for ref in refs[1:-1]:
        total = total + ref[...]
    total = total * (1.0 / math.sqrt(voxels))
    for jx in range(3):
        for jz in range(3):
            piece = total[(3 * jx + jz) * block_i : (3 * jx + jz + 1) * block_i]
            for jy in range(3):
                out[9 * jx + 3 * jy + jz] = piece[:, jy * block_o : (jy + 1) * block_o]


def local(inputs, cotangent, kernel):
    wx, wy, depth, chans = inputs.shape
    parts_x, parts_y = lax.axis_size("gx"), lax.axis_size("gy")
    size = parts_x * parts_y
    his, chips = parts_x // 2, parts_y // 2
    dims = (parts_x, parts_y, wx, wy, depth, chans)
    _, lo, _, _ = spot()
    rows, edge = wx * wy * depth, wy * depth // 2

    first = lax.dynamic_slice_in_dim(cotangent, lo * (wx - 1), 1, axis=0)
    second = lax.dynamic_slice_in_dim(cotangent, (1 - lo) * (wx - 1), 1, axis=0)
    outer = lax.ppermute(first, AXES, pairs_along(parts_x, parts_y, size, True))
    inner = lax.ppermute(second, AXES, pairs_along(parts_x, parts_y, size, False))
    values = inputs.astype(F32)
    act = (values * 0.5 * (1.0 + lax.erf(values / math.sqrt(2.0)))).astype(BF16)

    count = 2 * chips
    packed = call(
        functools.partial(pack_body, dims),
        [((rows + edge, chans), BF16)] * count + [(((wx + 2) * depth, chans), BF16)] * 2,
        (act, cotangent, outer, inner),
        flops=2 * count * (rows + edge) * 2 * chans * chans,
        moved=2 * (count + 3) * rows * chans,
    )
    masks = [a * parts_y + 2 * g for a in range(2) for g in range(chips)]
    same = [packed[0]] + [swap(packed[n], size, masks[n]) for n in range(1, count)]
    other = [swap(block, size, 1) for block in same]
    even = lax.ppermute(packed[count], AXES, pairs_along(parts_y, 1, size, False))
    odd = lax.ppermute(packed[count + 1], AXES, pairs_along(parts_y, 1, size, True))

    block_i, half = chans // parts_x, chans // 2
    total_y, total_x = wy * parts_y, 2 * wx
    raw = call(
        functools.partial(raw_body, dims),
        [((9 * block_i, chans), F32)] * his,
        (*same, *other),
        scratch=(
            pltpu.VMEM((total_x, total_y, depth, chans), BF16),
            pltpu.VMEM((3, total_x + 2, total_y + 2, depth, chans), BF16),
            pltpu.VMEM(((total_x + 2) * total_y * depth, chans), BF16),
            pltpu.VMEM((3 * half, 3 * chans), F32),
        ),
        flops=2 * total_x * total_y * depth * 9 * half * chans,
        moved=4 * count * rows * chans,
    )
    terms = [raw[0]] + [swap(raw[m], size, m * 2 * parts_y) for m in range(1, his)]
    (input_grad,) = call(
        functools.partial(back_body, dims),
        [((wx, wy, depth, chans), BF16)],
        (inputs, cotangent, outer, inner, even, odd, kernel),
        scratch=(pltpu.VMEM((wx + 2, wy + 2, depth, chans), BF16),),
        flops=2 * rows * 27 * chans * chans,
        moved=2 * 27 * chans * chans,
    )
    voxels = wx * parts_x * wy * parts_y * depth
    (kernel_grad,) = call(
        functools.partial(final_body, dims, voxels),
        [((27, block_i, chans // parts_y), F32)],
        terms,
        moved=4 * his * 9 * block_i * chans,
    )
    return (input_grad, kernel_grad)


def solution(mesh):
    return jax.shard_map(
        local,
        mesh=mesh,
        in_specs=(P("gx", "gy", None, None), P("gx", "gy", None, None), P()),
        out_specs=(P("gx", "gy", None, None), P(None, "gx", "gy")),
        check_vma=False,
    )
```

```python
import functools
import math

import jax
import jax.numpy as jnp
from jax import lax
from jax.experimental import pallas as pl
from jax.experimental.pallas import tpu as pltpu
from jax.sharding import PartitionSpec as P


AXES = ("gx", "gy")
BF16 = jnp.bfloat16
F32 = jnp.float32


def spot():
    at_x, at_y = lax.axis_index("gx"), lax.axis_index("gy")
    return at_x // 2, at_x % 2, at_y // 2, at_y % 2


def swap(array, size, mask):
    return lax.ppermute(array, AXES, [(i, i ^ mask) for i in range(size)])


def pairs_along(count, stride, size, odd):
    found = []
    for i in range(size):
        at = (i // stride) % count
        to = at ^ 1 if not odd else (at - 1 if at % 2 == 0 else at + 1)
        if 0 <= to < count:
            found.append((i, i + (to - at) * stride))
    return found


def call(body, outs, args, scratch=(), flops=0, moved=0):
    vmem = pl.BlockSpec(memory_space=pltpu.VMEM)
    return pl.pallas_call(
        body,
        out_shape=tuple(pltpu.VMEM(s, d) for s, d in outs),
        in_specs=[vmem] * len(args),
        out_specs=tuple(vmem for _ in outs),
        scratch_shapes=list(scratch),
        compiler_params=pltpu.CompilerParams(vmem_limit_bytes=32 << 20),
        cost_estimate=pl.CostEstimate(flops=flops, bytes_accessed=moved, transcendentals=0),
    )(*[pltpu.with_memory_space_constraint(a, pltpu.VMEM) for a in args])


def gelu_parts(values):
    cdf = 0.5 * (1.0 + lax.erf(values / math.sqrt(2.0)))
    return cdf


def pack_body(dims, inputs_ref, cot_ref, *outs):
    parts_x, parts_y, wx, wy, depth, chans = dims
    _, lo, chip, core = spot()
    chips = parts_y // 2
    block_i, half = chans // parts_x, chans // 2
    block_o = chans // parts_y
    rows = wx * wy * depth
    outs[-2][...] = cot_ref[lo * (wx - 1)].reshape(wy * depth, chans)
    outs[-1][...] = cot_ref[(1 - lo) * (wx - 1)].reshape(wy * depth, chans)
    values = inputs_ref[...].reshape(rows, chans).astype(F32)
    act = (values * gelu_parts(values)).astype(BF16)
    both = jnp.concatenate([act, cot_ref[...].reshape(rows, chans)], axis=1)
    lane = lax.broadcasted_iota(jnp.int32, (1, chans), 1)
    at = lax.broadcasted_iota(jnp.int32, (2 * chans, chans), 0)
    group = jnp.right_shift(lane, block_i.bit_length() - 1)
    column = lane - half
    side = jnp.right_shift(column, block_o.bit_length() - 1) ^ core
    for flip_lo in range(2):
        for flip in range(chips):
            to_lo, to_chip = lo ^ flip_lo, chip ^ flip
            from_act = (2 * group + to_lo) * block_i + (lane & (block_i - 1))
            from_cot = (2 * to_chip + side) * block_o + (column & (block_o - 1))
            from_cot = jnp.where(column < 2 * block_o, chans + from_cot, -1)
            chosen = (at == jnp.where(lane < half, from_act, from_cot)).astype(F32).astype(BF16)
            out = outs[flip_lo * chips + flip]
            out[...] = jnp.dot(both, chosen, preferred_element_type=F32).astype(BF16)


def rim_body(dims, cot_ref, outer_ref, inner_ref, even_ref, odd_ref):
    _, _, wx, wy, depth, _ = dims
    _, lo, _, core = spot()
    for out, column in ((even_ref, (1 - core) * (wy - 1)), (odd_ref, core * (wy - 1))):
        for x in range(wx):
            out[x + 1] = cot_ref[x, column]
        out[lo * (wx + 1)] = outer_ref[pl.ds(pl.multiple_of(column * depth, depth), depth)]
        out[(1 - lo) * (wx + 1)] = inner_ref[pl.ds(pl.multiple_of(column * depth, depth), depth)]


def in_lanes(value, shift, slot, width, lane):
    chans = value.shape[1]
    moved = pltpu.roll(value, shift % chans, 1) if shift % chans else value
    keep = (lane >= slot * width) & (lane < (slot + 1) * width)
    return jnp.where(keep, moved, 0.0).astype(BF16)


def unpack_body(dims, *refs):
    parts_x, parts_y, wx, wy, depth, chans = dims
    hi, lo, chip, core = spot()
    chips, half, block_o = parts_y // 2, chans // 2, chans // parts_y
    blocks = refs[: 4 * chips]
    acts, wide, even, odd, cots = refs[4 * chips :]
    total_y, strip = wy * parts_y, wy * depth
    lane = lax.broadcasted_iota(jnp.int32, (1, chans), 1)
    blank = jnp.zeros((depth, chans), BF16)
    for x in range(2 * wx):
        for slot in range(3):
            cots[slot, x, 0] = blank
            cots[slot, x, total_y + 1] = blank
    place = 0
    for flip_core in range(2):
        for flip_lo in range(2):
            for flip in range(chips):
                block = blocks[place]
                place += 1
                first_x = (lo ^ flip_lo) * wx
                first_y = (2 * (chip ^ flip) + (core ^ flip_core)) * wy
                for x in range(wx):
                    part = block[x * strip : (x + 1) * strip]
                    acts[first_x + x, pl.ds(first_y, wy)] = part.reshape(wy, depth, chans)
                    value = part.astype(F32)
                    for slot in range(3):
                        shift = (slot - flip_core) * block_o - half
                        cots[slot, first_x + x, pl.ds(first_y + 1, wy)] = in_lanes(
                            value, shift, slot, block_o, lane
                        ).reshape(wy, depth, chans)

    def merge(y, carry):
        for x in range(2 * wx):
            wide[x + 1, y] = cots[0, x, y + 2] + cots[1, x, y + 1] + cots[2, x, y]
        wide[0, y] = blank
        wide[2 * wx + 1, y] = blank
        return carry

    lax.fori_loop(0, total_y, merge, 0, unroll=4)
    part_y = total_y // 4
    size = part_y * depth
    for out, x in ((even, (1 - hi % 2) * (2 * wx - 1)), (odd, (hi % 2) * (2 * wx - 1))):
        total = cots[0, x, 1 : 1 + part_y] + cots[1, x, 1 + part_y : 1 + 2 * part_y]
        total = total + cots[2, x, 1 + 2 * part_y : 1 + 3 * part_y]
        last = cots[0, x, 1 + 3 * part_y : 1 + 4 * part_y].reshape(size, chans).astype(F32)
        last = pltpu.roll(last, 3 * block_o, 1).astype(BF16)
        out[...] = total.reshape(size, chans) + last


def main_body(dims, acts, wide, sums, low, high):
    parts_x, parts_y, wx, wy, depth, chans = dims
    half, total_y = chans // 2, wy * parts_y
    step = min(total_y, 16)
    z = lax.broadcasted_iota(jnp.int32, (depth, 1), 0)
    sums[...] = jnp.zeros_like(sums)
    for x in range(2 * wx):

        def chunk(n, carry, x=x):
            planes = pl.ds(n * step, step)
            middle = acts[x, planes][:, :, :half].astype(F32)
            below = jnp.where(z > 0, pltpu.roll(middle, 1, 1), 0.0)
            above = jnp.where(z < depth - 1, pltpu.roll(middle, depth - 1, 1), 0.0)
            left = jnp.concatenate([below, middle, above], axis=2).astype(BF16)
            left = left.reshape(step * depth, 3 * half)
            if x == 0:
                low[pl.ds(pl.multiple_of(n * step * depth, step * depth), step * depth)] = left
            if x == 2 * wx - 1:
                high[pl.ds(pl.multiple_of(n * step * depth, step * depth), step * depth)] = left
            right = jnp.concatenate(
                [wide[x + 2 - jx, planes].reshape(step * depth, chans) for jx in range(3)], axis=1
            )
            sums[...] += lax.dot_general(
                left, right, (((0,), (0,)), ((), ())), preferred_element_type=F32
            )
            return carry

        if total_y == step:
            chunk(0, 0)
        else:
            lax.fori_loop(0, total_y // step, chunk, 0)


def ends_body(dims, main_ref, low, high, even, odd, *refs):
    parts_x, parts_y, wx, wy, depth, chans = dims
    hi, _, _, _ = spot()
    his = parts_x // 2
    block_i, half, block_o = chans // parts_x, chans // 2, chans // parts_y
    outs, (cots, sums) = refs[:his], refs[his:]
    total_y = wy * parts_y
    part_y = total_y // 4
    size = part_y * depth
    lane = lax.broadcasted_iota(jnp.int32, (1, chans), 1)
    blank = jnp.zeros((depth, chans), BF16)
    for end in range(2):
        for slot in range(3):
            cots[end, slot, 0] = blank
            cots[end, slot, total_y + 1] = blank
    for ref, end in ((even, 1 - hi % 2), (odd, hi % 2)):
        value = ref[...].astype(F32)
        for slot in range(3):
            for part in range(4):
                cots[end, slot, 1 + part * part_y : 1 + (part + 1) * part_y] = in_lanes(
                    value, (slot - part) * block_o, slot, block_o, lane
                ).reshape(part_y, depth, chans)
    sums[...] = main_ref[...]
    for end, left, jx in ((0, low, 2), (1, high, 0)):
        right = cots[end, 0, 2 : total_y + 2] + cots[end, 1, 1 : total_y + 1]
        right = right + cots[end, 2, 0:total_y]
        sums[:, jx * chans : (jx + 1) * chans] += lax.dot_general(
            left[...],
            right.reshape(total_y * depth, chans),
            (((0,), (0,)), ((), ())),
            preferred_element_type=F32,
        )
    free = 3 * block_o
    for flip, out in enumerate(outs):
        start = pl.multiple_of((hi ^ flip) * block_i, block_i)

        def group(jx, jz):
            return sums[pl.ds(jz * half + start, block_i), jx * chans : (jx + 1) * chans]

        last = jnp.zeros((block_i, chans), F32)
        for jz in range(3):
            spare = group(2, jz)
            for jx in range(2):
                moved = pltpu.roll(spare, free - jx * block_o, 1)
                piece = jnp.where(lane < free, group(jx, jz), moved)
                out[(3 * jx + jz) * block_i : (3 * jx + jz + 1) * block_i] = piece.astype(out.dtype)
            moved = pltpu.roll(spare, ((jz - 2) * block_o) % chans, 1)
            keep = (lane >= jz * block_o) & (lane < (jz + 1) * block_o)
            last = jnp.where(keep, moved, last)
        out[6 * block_i :] = last.astype(out.dtype)


def back_body(dims, inputs_ref, cot_ref, outer_ref, inner_ref, even_ref, odd_ref, kernel_ref, out_ref, pad):
    _, _, wx, wy, depth, chans = dims
    _, lo, _, core = spot()
    rows = wx * wy * depth
    pad[1 : wx + 1, 1 : wy + 1] = cot_ref[...]
    pad[(1 - lo) * (wx + 1), 1 : wy + 1] = inner_ref[...].reshape(wy, depth, chans)
    pad[lo * (wx + 1), 1 : wy + 1] = outer_ref[...].reshape(wy, depth, chans)
    even, odd = (1 - core) * (wy + 1), core * (wy + 1)
    for x in range(wx + 2):
        pad[x, even] = even_ref[x]
        pad[x, odd] = odd_ref[x]
    left, right = [], []
    for jx in range(3):
        for jy in range(3):
            first = jx * 9 + jy * 3
            piece = pad[2 - jx : 2 - jx + wx, 2 - jy : 2 - jy + wy]
            left.append(piece.reshape(rows, chans))
            right.append(kernel_ref[first : first + 3].reshape(3 * chans, chans))
    product = lax.dot_general(
        jnp.concatenate(left, axis=1),
        jnp.concatenate(right, axis=1),
        (((1,), (1,)), ((), ())),
        preferred_element_type=F32,
    ).reshape(wx * wy, depth, 3 * chans)
    z = lax.broadcasted_iota(jnp.int32, (depth, 1), 0)
    low = product[:, :, :chans]
    high = product[:, :, 2 * chans :]
    back = product[:, :, chans : 2 * chans]
    back += jnp.where(z < depth - 1, pltpu.roll(low, depth - 1, 1), 0.0)
    back += jnp.where(z > 0, pltpu.roll(high, 1, 1), 0.0)
    values = inputs_ref[...].astype(F32).reshape(wx * wy, depth, chans)
    cdf = gelu_parts(values)
    slope = cdf + values * jnp.exp(-0.5 * values * values) / math.sqrt(2.0 * math.pi)
    out_ref[...] = (slope * back).astype(BF16).reshape(wx, wy, depth, chans)


def final_body(dims, voxels, *refs):
    parts_x, parts_y, _, _, _, chans = dims
    block_i, block_o = chans // parts_x, chans // parts_y
    out = refs[-1]
    total = refs[0][...]
    for ref in refs[1:-1]:
        total = total + ref[...].astype(F32)
    total = total * (1.0 / math.sqrt(voxels))
    for jx in range(3):
        for jy in range(3):
            for jz in range(3):
                if jx < 2:
                    row, column = 3 * jx + jz, jy
                elif jy < 2:
                    row, column = 3 * jy + jz, 3
                else:
                    row, column = 6, jz
                out[9 * jx + 3 * jy + jz] = total[
                    row * block_i : (row + 1) * block_i, column * block_o : (column + 1) * block_o
                ]


def local(inputs, cotangent, kernel):
    wx, wy, depth, chans = inputs.shape
    parts_x, parts_y = lax.axis_size("gx"), lax.axis_size("gy")
    size = parts_x * parts_y
    his, chips = parts_x // 2, parts_y // 2
    dims = (parts_x, parts_y, wx, wy, depth, chans)
    rows = wx * wy * depth
    block_i, half = chans // parts_x, chans // 2
    total_y, total_x = wy * parts_y, 2 * wx
    face = (wy * depth, chans)

    count = 2 * chips
    *packed, outer, inner = call(
        functools.partial(pack_body, dims),
        [((rows, chans), BF16)] * count + [(face, BF16)] * 2,
        (inputs, cotangent),
        flops=2 * count * rows * 2 * chans * chans,
        moved=2 * (count + 3) * rows * chans,
    )
    masks = [a * parts_y + 2 * g for a in range(2) for g in range(chips)]
    same = [packed[0]] + [swap(packed[n], size, masks[n]) for n in range(1, count)]
    other = [swap(block, size, 1) for block in same]
    outer = lax.ppermute(outer, AXES, pairs_along(parts_x, parts_y, size, True))
    inner = lax.ppermute(inner, AXES, pairs_along(parts_x, parts_y, size, False))
    even, odd = call(
        functools.partial(rim_body, dims),
        [((wx + 2, depth, chans), BF16)] * 2,
        (cotangent, outer, inner),
    )
    even = lax.ppermute(even, AXES, pairs_along(parts_y, 1, size, False))
    odd = lax.ppermute(odd, AXES, pairs_along(parts_y, 1, size, True))

    acts, wide, end_even, end_odd = call(
        functools.partial(unpack_body, dims),
        [
            ((total_x, total_y, depth, chans), BF16),
            ((total_x + 2, total_y, depth, chans), BF16),
            ((total_y // 4 * depth, chans), BF16),
            ((total_y // 4 * depth, chans), BF16),
        ],
        (*same, *other),
        scratch=(pltpu.VMEM((3, total_x, total_y + 2, depth, chans), BF16),),
        moved=4 * count * rows * chans,
    )
    end_even = lax.ppermute(end_even, AXES, pairs_along(his, 2 * parts_y, size, False))
    end_odd = lax.ppermute(end_odd, AXES, pairs_along(his, 2 * parts_y, size, True))
    sums, low, high = call(
        functools.partial(main_body, dims),
        [((3 * half, 3 * chans), F32), ((total_y * depth, 3 * half), BF16), ((total_y * depth, 3 * half), BF16)],
        (acts, wide),
        flops=2 * total_x * total_y * depth * 9 * half * chans,
        moved=4 * count * rows * chans,
    )
    raw = call(
        functools.partial(ends_body, dims),
        [((7 * block_i, chans), BF16 if m else F32) for m in range(his)],
        (sums, low, high, end_even, end_odd),
        scratch=(
            pltpu.VMEM((2, 3, total_y + 2, depth, chans), BF16),
            pltpu.VMEM((3 * half, 3 * chans), F32),
        ),
        flops=4 * total_y * depth * 3 * half * chans,
        moved=4 * total_y * depth * chans,
    )
    terms = [raw[0]] + [swap(raw[m], size, m * 2 * parts_y) for m in range(1, his)]
    (input_grad,) = call(
        functools.partial(back_body, dims),
        [((wx, wy, depth, chans), BF16)],
        (inputs, cotangent, outer, inner, even, odd, kernel),
        scratch=(pltpu.VMEM((wx + 2, wy + 2, depth, chans), BF16),),
        flops=2 * rows * 27 * chans * chans,
        moved=2 * 27 * chans * chans,
    )
    voxels = wx * parts_x * wy * parts_y * depth
    (kernel_grad,) = call(
        functools.partial(final_body, dims, voxels),
        [((27, block_i, chans // parts_y), F32)],
        terms,
        moved=4 * his * 7 * block_i * chans,
    )
    return (input_grad, kernel_grad)


def solution(mesh):
    return jax.shard_map(
        local,
        mesh=mesh,
        in_specs=(P("gx", "gy", None, None), P("gx", "gy", None, None), P()),
        out_specs=(P("gx", "gy", None, None), P(None, "gx", "gy")),
        check_vma=False,
    )
```

```python
import functools
import math

import jax
import jax.numpy as jnp
from jax import lax
from jax.experimental import pallas as pl
from jax.experimental.pallas import tpu as pltpu
from jax.sharding import PartitionSpec as P


AXES = ("gx", "gy")
BF16 = jnp.bfloat16
F32 = jnp.float32


def near_flips(chips):
    return [(1 << k) - 1 for k in range(1, chips.bit_length())]


def spot():
    at_x, at_y = lax.axis_index("gx"), lax.axis_index("gy")
    return at_x // 2, at_x % 2, at_y // 2, at_y % 2


def move(array, pairs):
    return lax.ppermute(array, AXES, pairs)


def swap(array, size, mask):
    return move(array, [(i, i ^ mask) for i in range(size)])


def pairs_along(count, stride, size, odd):
    found = []
    for i in range(size):
        at = (i // stride) % count
        to = at ^ 1 if not odd else (at - 1 if at % 2 == 0 else at + 1)
        if 0 <= to < count:
            found.append((i, i + (to - at) * stride))
    return found


def call(body, outs, args, scratch=(), flops=0, moved=0, fetch=False):
    vmem = pl.BlockSpec(memory_space=pltpu.VMEM)
    run = pl.pallas_call(
        body,
        out_shape=tuple(pltpu.VMEM(s, d) for s, d in outs),
        in_specs=[pl.BlockSpec(memory_space=pltpu.HBM) if fetch else vmem] * len(args),
        out_specs=tuple(vmem for _ in outs),
        scratch_shapes=list(scratch),
        compiler_params=pltpu.CompilerParams(vmem_limit_bytes=32 << 20),
        cost_estimate=pl.CostEstimate(flops=flops, bytes_accessed=moved, transcendentals=0),
    )
    space = pltpu.HBM if fetch else pltpu.VMEM
    args = [pltpu.with_memory_space_constraint(a, space) for a in args]
    return run(*args)


def gelu_parts(values):
    cdf = 0.5 * (1.0 + lax.erf(values / math.sqrt(2.0)))
    return cdf


def pack_body(dims, inputs_hbm, cot_hbm, *refs):
    parts_x, parts_y, wx, wy, depth, chans = dims
    _, lo, chip, core = spot()
    chips = parts_y // 2
    block_i, half = chans // parts_x, chans // 2
    block_o = chans // parts_y
    rows = wx * wy * depth
    *outs, inputs_ref, cot_ref, arrived = refs
    copies = [
        pltpu.make_async_copy(inputs_hbm, inputs_ref, arrived.at[0]),
        pltpu.make_async_copy(cot_hbm, cot_ref, arrived.at[1]),
    ]
    for copy in copies:
        copy.start()
    for copy in copies:
        copy.wait()
    outs[-2][...] = cot_ref[lo * (wx - 1)].reshape(wy * depth, chans)
    outs[-1][...] = cot_ref[(1 - lo) * (wx - 1)].reshape(wy * depth, chans)
    for flip in [0, *near_flips(chips)]:
        column = (core if flip else 1 - core) * (wy - 1)
        for x in range(wx):
            plane = cot_ref[x, column]
            outs[flip][rows + x * depth : rows + (x + 1) * depth] = plane
            outs[chips + flip][rows + x * depth : rows + (x + 1) * depth] = plane
    values = inputs_ref[...].reshape(rows, chans).astype(F32)
    act = (values * gelu_parts(values)).astype(BF16)
    both = jnp.concatenate([act, cot_ref[...].reshape(rows, chans)], axis=1)
    lane = lax.broadcasted_iota(jnp.int32, (1, chans), 1)
    at = lax.broadcasted_iota(jnp.int32, (2 * chans, chans), 0)
    group = jnp.right_shift(lane, block_i.bit_length() - 1)
    column = lane - half
    side = jnp.right_shift(column, block_o.bit_length() - 1) ^ core
    for flip_lo in range(2):
        for flip in range(chips):
            to_lo, to_chip = lo ^ flip_lo, chip ^ flip
            from_act = (2 * group + to_lo) * block_i + (lane & (block_i - 1))
            from_cot = (2 * to_chip + side) * block_o + (column & (block_o - 1))
            from_cot = jnp.where(column < 2 * block_o, chans + from_cot, -1)
            chosen = (at == jnp.where(lane < half, from_act, from_cot)).astype(F32).astype(BF16)
            out = outs[flip_lo * chips + flip]
            out[:rows] = jnp.dot(both, chosen, preferred_element_type=F32).astype(BF16)


def in_lanes(value, shift, slot, width, lane):
    chans = value.shape[1]
    moved = pltpu.roll(value, shift % chans, 1) if shift % chans else value
    keep = (lane >= slot * width) & (lane < (slot + 1) * width)
    return jnp.where(keep, moved, 0.0).astype(BF16)


def unpack_body(dims, *refs):
    _, parts_y, wx, wy, depth, chans = dims
    hi, lo, chip, core = spot()
    chips, half, block_o = parts_y // 2, chans // 2, chans // parts_y
    blocks, cot_ref = refs[: 4 * chips], refs[4 * chips]
    acts, wide, even, odd, pad, cots = refs[4 * chips + 1 :]
    rows = wx * wy * depth
    total_y, strip = wy * parts_y, wy * depth
    lane = lax.broadcasted_iota(jnp.int32, (1, chans), 1)
    blank = jnp.zeros((depth, chans), BF16)
    for x in range(2 * wx):
        for slot in range(3):
            cots[slot, x, 0] = blank
            cots[slot, x, total_y + 1] = blank
    facing = (1 - lo) * (wx + 1)
    toward, away = (1 - core) * (wy + 1), core * (wy + 1)
    swapped = blocks[2 * chips :]
    pad[1 : wx + 1, 1 : wy + 1] = cot_ref[...]
    near_row = pl.multiple_of(rows + lo * (wx - 1) * depth, depth)
    far_row = pl.multiple_of(rows + (1 - lo) * (wx - 1) * depth, depth)
    size = total_y // 4 * depth
    pad[facing, toward] = swapped[chips][pl.ds(near_row, depth)]
    pad[facing, away] = blank
    for out in (even, odd):
        out[size : size + depth] = swapped[chips][pl.ds(far_row, depth)]
        out[size + depth :] = blank
    for x in range(wx):
        pad[x + 1, toward] = swapped[0][rows + x * depth : rows + (x + 1) * depth]
        pad[x + 1, away] = blank
    for flip in near_flips(chips):

        @pl.when((chip ^ flip) == chip + 2 * core - 1)
        def _(flip=flip):
            pad[facing, away] = swapped[chips + flip][pl.ds(near_row, depth)]
            for out in (even, odd):
                out[size + depth :] = swapped[chips + flip][pl.ds(far_row, depth)]
            for x in range(wx):
                pad[x + 1, away] = swapped[flip][rows + x * depth : rows + (x + 1) * depth]

    place = 0
    for flip_core in range(2):
        for flip_lo in range(2):
            for flip in range(chips):
                block = blocks[place]
                place += 1
                first_x = (lo ^ flip_lo) * wx
                first_y = (2 * (chip ^ flip) + (core ^ flip_core)) * wy
                for x in range(wx):
                    part = block[x * strip : (x + 1) * strip]
                    acts[first_x + x, pl.ds(first_y, wy)] = part.reshape(wy, depth, chans)
                    value = part.astype(F32)
                    for slot in range(3):
                        shift = (slot - flip_core) * block_o - half
                        cots[slot, first_x + x, pl.ds(first_y + 1, wy)] = in_lanes(
                            value, shift, slot, block_o, lane
                        ).reshape(wy, depth, chans)

    def merge(y, carry):
        for x in range(2 * wx):
            wide[x + 1, y] = cots[0, x, y + 2] + cots[1, x, y + 1] + cots[2, x, y]
        wide[0, y] = blank
        wide[2 * wx + 1, y] = blank
        return carry

    lax.fori_loop(0, total_y, merge, 0, unroll=4)
    part_y = total_y // 4
    for out, x in ((even, (1 - hi % 2) * (2 * wx - 1)), (odd, (hi % 2) * (2 * wx - 1))):
        total = cots[0, x, 1 : 1 + part_y] + cots[1, x, 1 + part_y : 1 + 2 * part_y]
        total = total + cots[2, x, 1 + 2 * part_y : 1 + 3 * part_y]
        last = cots[0, x, 1 + 3 * part_y : 1 + 4 * part_y].reshape(size, chans).astype(F32)
        last = pltpu.roll(last, 3 * block_o, 1).astype(BF16)
        out[:size] = total.reshape(size, chans) + last


def main_body(dims, acts, wide, sums, low, high):
    _, parts_y, wx, wy, depth, chans = dims
    half, total_y = chans // 2, wy * parts_y
    step = min(total_y, 16)
    z = lax.broadcasted_iota(jnp.int32, (depth, 1), 0)
    sums[...] = jnp.zeros_like(sums)
    for x in range(2 * wx):

        def chunk(n, carry, x=x):
            planes = pl.ds(n * step, step)
            middle = acts[x, planes][:, :, :half].astype(F32)
            below = jnp.where(z > 0, pltpu.roll(middle, 1, 1), 0.0)
            above = jnp.where(z < depth - 1, pltpu.roll(middle, depth - 1, 1), 0.0)
            left = jnp.concatenate([below, middle, above], axis=2).astype(BF16)
            left = left.reshape(step * depth, 3 * half)
            if x == 0:
                low[pl.ds(pl.multiple_of(n * step * depth, step * depth), step * depth)] = left
            if x == 2 * wx - 1:
                high[pl.ds(pl.multiple_of(n * step * depth, step * depth), step * depth)] = left
            right = jnp.concatenate(
                [wide[x + 2 - jx, planes].reshape(step * depth, chans) for jx in range(3)], axis=1
            )
            sums[...] += lax.dot_general(
                left, right, (((0,), (0,)), ((), ())), preferred_element_type=F32
            )
            return carry

        if total_y == step:
            chunk(0, 0)
        else:
            lax.fori_loop(0, total_y // step, chunk, 0)


def ends_body(dims, main_ref, low, high, even, odd, *refs):
    parts_x, parts_y, _, wy, depth, chans = dims
    hi, _, _, _ = spot()
    his = parts_x // 2
    block_i, half, block_o = chans // parts_x, chans // 2, chans // parts_y
    outs, (cots, sums) = refs[:his], refs[his:]
    total_y = wy * parts_y
    part_y = total_y // 4
    size = part_y * depth
    lane = lax.broadcasted_iota(jnp.int32, (1, chans), 1)
    blank = jnp.zeros((depth, chans), BF16)
    for end in range(2):
        for slot in range(3):
            cots[end, slot, 0] = blank
            cots[end, slot, total_y + 1] = blank
    for ref, end in ((even, 1 - hi % 2), (odd, hi % 2)):
        value = ref[:size].astype(F32)
        for slot in range(3):
            for part in range(4):
                cots[end, slot, 1 + part * part_y : 1 + (part + 1) * part_y] = in_lanes(
                    value, (slot - part) * block_o, slot, block_o, lane
                ).reshape(part_y, depth, chans)
    sums[...] = main_ref[...]
    for end, left, jx in ((0, low, 2), (1, high, 0)):
        right = cots[end, 0, 2 : total_y + 2] + cots[end, 1, 1 : total_y + 1]
        right = right + cots[end, 2, 0:total_y]
        sums[:, jx * chans : (jx + 1) * chans] += lax.dot_general(
            left[...],
            right.reshape(total_y * depth, chans),
            (((0,), (0,)), ((), ())),
            preferred_element_type=F32,
        )
    free = 3 * block_o
    for flip, out in enumerate(outs):
        start = pl.multiple_of((hi ^ flip) * block_i, block_i)

        def group(jx, jz):
            return sums[pl.ds(jz * half + start, block_i), jx * chans : (jx + 1) * chans]

        last = jnp.zeros((block_i, chans), F32)
        for jz in range(3):
            spare = group(2, jz)
            for jx in range(2):
                moved = pltpu.roll(spare, free - jx * block_o, 1)
                piece = jnp.where(lane < free, group(jx, jz), moved)
                out[(3 * jx + jz) * block_i : (3 * jx + jz + 1) * block_i] = piece.astype(out.dtype)
            moved = pltpu.roll(spare, ((jz - 2) * block_o) % chans, 1)
            keep = (lane >= jz * block_o) & (lane < (jz + 1) * block_o)
            last = jnp.where(keep, moved, last)
        out[6 * block_i :] = last.astype(out.dtype)


def back_body(dims, inputs_ref, pad_ref, outer_ref, inner_ref, even, odd, kernel_ref, out_ref, pad):
    _, parts_y, wx, wy, depth, chans = dims
    hi, lo, _, core = spot()
    rows = wx * wy * depth
    pad[...] = pad_ref[...]
    pad[(1 - lo) * (wx + 1), 1 : wy + 1] = inner_ref[...].reshape(wy, depth, chans)
    pad[lo * (wx + 1), 1 : wy + 1] = outer_ref[...].reshape(wy, depth, chans)
    toward, away = (1 - core) * (wy + 1), core * (wy + 1)
    size = wy * parts_y // 4 * depth
    for ref, parity in ((even, 1), (odd, 0)):

        @pl.when((hi + lo) % 2 == parity)
        def _(ref=ref):
            pad[lo * (wx + 1), toward] = ref[size : size + depth]
            pad[lo * (wx + 1), away] = ref[size + depth :]

    left, right = [], []
    for jx in range(3):
        for jy in range(3):
            first = jx * 9 + jy * 3
            piece = pad[2 - jx : 2 - jx + wx, 2 - jy : 2 - jy + wy]
            left.append(piece.reshape(rows, chans))
            right.append(kernel_ref[first : first + 3].reshape(3 * chans, chans))
    product = lax.dot_general(
        jnp.concatenate(left, axis=1),
        jnp.concatenate(right, axis=1),
        (((1,), (1,)), ((), ())),
        preferred_element_type=F32,
    ).reshape(wx * wy, depth, 3 * chans)
    z = lax.broadcasted_iota(jnp.int32, (depth, 1), 0)
    low = product[:, :, :chans]
    high = product[:, :, 2 * chans :]
    back = product[:, :, chans : 2 * chans]
    back += jnp.where(z < depth - 1, pltpu.roll(low, depth - 1, 1), 0.0)
    back += jnp.where(z > 0, pltpu.roll(high, 1, 1), 0.0)
    values = inputs_ref[...].astype(F32).reshape(wx * wy, depth, chans)
    cdf = gelu_parts(values)
    slope = cdf + values * jnp.exp(-0.5 * values * values) / math.sqrt(2.0 * math.pi)
    out_ref[...] = (slope * back).astype(BF16).reshape(wx, wy, depth, chans)


def final_body(dims, voxels, *refs):
    parts_x, parts_y, _, _, _, chans = dims
    block_i, block_o = chans // parts_x, chans // parts_y
    out = refs[-1]
    total = refs[0][...]
    for ref in refs[1:-1]:
        total = total + ref[...].astype(F32)
    total = total * (1.0 / math.sqrt(voxels))
    for jx in range(3):
        for jy in range(3):
            for jz in range(3):
                if jx < 2:
                    row, column = 3 * jx + jz, jy
                elif jy < 2:
                    row, column = 3 * jy + jz, 3
                else:
                    row, column = 6, jz
                out[9 * jx + 3 * jy + jz] = total[
                    row * block_i : (row + 1) * block_i, column * block_o : (column + 1) * block_o
                ]


def local(inputs, cotangent, kernel):
    wx, wy, depth, chans = inputs.shape
    parts_x, parts_y = lax.axis_size("gx"), lax.axis_size("gy")
    size = parts_x * parts_y
    his, chips = parts_x // 2, parts_y // 2
    dims = (parts_x, parts_y, wx, wy, depth, chans)
    rows = wx * wy * depth
    block_i, half = chans // parts_x, chans // 2
    total_y, total_x = wy * parts_y, 2 * wx
    face = (wy * depth, chans)
    near = [0, *near_flips(chips)]
    extras = [rows + wx * depth * (n % chips in near) for n in range(2 * chips)]

    count = 2 * chips
    *packed, outer, inner = call(
        functools.partial(pack_body, dims),
        [((n, chans), BF16) for n in extras] + [(face, BF16)] * 2,
        (inputs, cotangent),
        scratch=(
            pltpu.VMEM(inputs.shape, BF16),
            pltpu.VMEM(inputs.shape, BF16),
            pltpu.SemaphoreType.DMA((2,)),
        ),
        fetch=True,
        flops=2 * count * rows * 2 * chans * chans,
        moved=2 * (count + 3) * rows * chans,
    )
    masks = [a * parts_y + 2 * g for a in range(2) for g in range(chips)]
    same = [packed[0]] + [swap(packed[n], size, masks[n]) for n in range(1, count)]
    other = [swap(same[n], size, 1) for n in range(count)]
    outer = move(outer, pairs_along(parts_x, parts_y, size, True))
    inner = move(inner, pairs_along(parts_x, parts_y, size, False))

    acts, wide, end_even, end_odd, pad = call(
        functools.partial(unpack_body, dims),
        [
            ((total_x, total_y, depth, chans), BF16),
            ((total_x + 2, total_y, depth, chans), BF16),
            (((total_y // 4 + 2) * depth, chans), BF16),
            (((total_y // 4 + 2) * depth, chans), BF16),
            ((wx + 2, wy + 2, depth, chans), BF16),
        ],
        (*same, *other, cotangent),
        scratch=(pltpu.VMEM((3, total_x, total_y + 2, depth, chans), BF16),),
        moved=4 * count * rows * chans,
    )
    end_even = move(end_even, pairs_along(his, 2 * parts_y, size, False))
    end_odd = move(end_odd, pairs_along(his, 2 * parts_y, size, True))
    sums, low, high = call(
        functools.partial(main_body, dims),
        [((3 * half, 3 * chans), F32), ((total_y * depth, 3 * half), BF16), ((total_y * depth, 3 * half), BF16)],
        (acts, wide),
        flops=2 * total_x * total_y * depth * 9 * half * chans,
        moved=4 * count * rows * chans,
    )
    raw = call(
        functools.partial(ends_body, dims),
        [((7 * block_i, chans), BF16 if m else F32) for m in range(his)],
        (sums, low, high, end_even, end_odd),
        scratch=(
            pltpu.VMEM((2, 3, total_y + 2, depth, chans), BF16),
            pltpu.VMEM((3 * half, 3 * chans), F32),
        ),
        flops=4 * total_y * depth * 3 * half * chans,
        moved=4 * total_y * depth * chans,
    )
    terms = [raw[0]] + [swap(raw[m], size, m * 2 * parts_y) for m in range(1, his)]
    (input_grad,) = call(
        functools.partial(back_body, dims),
        [((wx, wy, depth, chans), BF16)],
        (inputs, pad, outer, inner, end_even, end_odd, kernel),
        scratch=(pltpu.VMEM((wx + 2, wy + 2, depth, chans), BF16),),
        flops=2 * rows * 27 * chans * chans,
        moved=2 * 27 * chans * chans,
    )
    voxels = wx * parts_x * wy * parts_y * depth
    (kernel_grad,) = call(
        functools.partial(final_body, dims, voxels),
        [((27, block_i, chans // parts_y), F32)],
        terms,
        moved=4 * his * 7 * block_i * chans,
    )
    return (input_grad, kernel_grad)


def solution(mesh):
    return jax.shard_map(
        local,
        mesh=mesh,
        in_specs=(P("gx", "gy", None, None), P("gx", "gy", None, None), P()),
        out_specs=(P("gx", "gy", None, None), P(None, "gx", "gy")),
        check_vma=False,
    )
```

```python
import functools
import math

import jax
import jax.numpy as jnp
from jax import lax
from jax.experimental import pallas as pl
from jax.experimental.pallas import tpu as pltpu
from jax.sharding import PartitionSpec as P


AXES = ("gx", "gy")
BF16 = jnp.bfloat16
F32 = jnp.float32


def near_flips(chips):
    return [(1 << k) - 1 for k in range(1, chips.bit_length())]


def spot():
    at_x, at_y = lax.axis_index("gx"), lax.axis_index("gy")
    return at_x // 2, at_x % 2, at_y // 2, at_y % 2


def move(array, pairs):
    return lax.ppermute(array, AXES, pairs)


def swap(array, size, mask):
    return move(array, [(i, i ^ mask) for i in range(size)])


def pairs_along(count, stride, size, odd):
    found = []
    for i in range(size):
        at = (i // stride) % count
        to = at ^ 1 if not odd else (at - 1 if at % 2 == 0 else at + 1)
        if 0 <= to < count:
            found.append((i, i + (to - at) * stride))
    return found


def call(body, outs, args, scratch=(), flops=0, moved=0, fetch=False, last=False):
    vmem = pl.BlockSpec(memory_space=pltpu.VMEM)
    run = pl.pallas_call(
        body,
        out_shape=tuple((jax.ShapeDtypeStruct if last else pltpu.VMEM)(s, d) for s, d in outs),
        in_specs=[pl.BlockSpec(memory_space=pltpu.HBM) if fetch else vmem] * len(args),
        out_specs=tuple(vmem for _ in outs),
        scratch_shapes=list(scratch),
        compiler_params=pltpu.CompilerParams(vmem_limit_bytes=32 << 20),
        cost_estimate=pl.CostEstimate(flops=flops, bytes_accessed=moved, transcendentals=0),
    )
    space = pltpu.HBM if fetch else pltpu.VMEM
    args = [pltpu.with_memory_space_constraint(a, space) for a in args]
    return run(*args)


def gelu_parts(values):
    cdf = 0.5 * (1.0 + lax.erf(values / math.sqrt(2.0)))
    return cdf


def pack_body(dims, inputs_hbm, cot_hbm, *refs):
    parts_x, parts_y, wx, wy, depth, chans = dims
    _, lo, chip, core = spot()
    chips = parts_y // 2
    block_i, half = chans // parts_x, chans // 2
    block_o = chans // parts_y
    rows = wx * wy * depth
    *outs, inputs_ref, cot_ref, arrived = refs
    copies = [
        pltpu.make_async_copy(inputs_hbm, inputs_ref, arrived.at[0]),
        pltpu.make_async_copy(cot_hbm, cot_ref, arrived.at[1]),
    ]
    for copy in copies:
        copy.start()
    for copy in copies:
        copy.wait()
    outs[-2][...] = cot_ref[lo * (wx - 1)].reshape(wy * depth, chans)
    outs[-1][...] = cot_ref[(1 - lo) * (wx - 1)].reshape(wy * depth, chans)
    for flip in [0, *near_flips(chips)]:
        column = (core if flip else 1 - core) * (wy - 1)
        for x in range(wx):
            plane = cot_ref[x, column]
            outs[flip][rows + x * depth : rows + (x + 1) * depth] = plane
            outs[chips + flip][rows + x * depth : rows + (x + 1) * depth] = plane
    values = inputs_ref[...].reshape(rows, chans).astype(F32)
    act = (values * gelu_parts(values)).astype(BF16)
    both = jnp.concatenate([act, cot_ref[...].reshape(rows, chans)], axis=1)
    lane = lax.broadcasted_iota(jnp.int32, (1, chans), 1)
    at = lax.broadcasted_iota(jnp.int32, (2 * chans, chans), 0)
    group = jnp.right_shift(lane, block_i.bit_length() - 1)
    column = lane - half
    side = jnp.right_shift(column, block_o.bit_length() - 1) ^ core
    for flip_lo in range(2):
        for flip in range(chips):
            to_lo, to_chip = lo ^ flip_lo, chip ^ flip
            from_act = (2 * group + to_lo) * block_i + (lane & (block_i - 1))
            from_cot = (2 * to_chip + side) * block_o + (column & (block_o - 1))
            from_cot = jnp.where(column < 2 * block_o, chans + from_cot, -1)
            chosen = (at == jnp.where(lane < half, from_act, from_cot)).astype(F32).astype(BF16)
            out = outs[flip_lo * chips + flip]
            out[:rows] = jnp.dot(both, chosen, preferred_element_type=F32).astype(BF16)


def in_lanes(value, shift, slot, width, lane):
    chans = value.shape[1]
    moved = pltpu.roll(value, shift % chans, 1) if shift % chans else value
    keep = (lane >= slot * width) & (lane < (slot + 1) * width)
    return jnp.where(keep, moved, 0.0).astype(BF16)


def edges_body(dims, *refs):
    _, parts_y, wx, wy, depth, chans = dims
    hi, lo, chip, core = spot()
    chips, half, block_o = parts_y // 2, chans // 2, chans // parts_y
    blocks, outs = refs[: 4 * chips], refs[4 * chips :]
    swapped = blocks[2 * chips :]
    strip, quarter = wy * depth, parts_y // 4
    rows, size = wx * strip, quarter * strip
    lane = lax.broadcasted_iota(jnp.int32, (1, chans), 1)
    far_row = pl.multiple_of(rows + (1 - lo) * (wx - 1) * depth, depth)
    for out in outs:
        out[size : size + depth] = swapped[chips][pl.ds(far_row, depth)]
        out[size + depth :] = jnp.zeros((depth, chans), BF16)
    for flip in near_flips(chips):

        @pl.when((chip ^ flip) == chip + 2 * core - 1)
        def _(flip=flip):
            for out in outs:
                out[size + depth :] = swapped[chips + flip][pl.ds(far_row, depth)]

    for flip_lo in range(2):
        from_lo = lo ^ flip_lo
        row = pl.multiple_of(from_lo * (wx - 1) * strip, strip)
        pieces = {}
        for flip_core in range(2):
            for flip in range(chips):
                block = blocks[(2 * flip_core + flip_lo) * chips + flip]
                from_y = 2 * (chip ^ flip) + (core ^ flip_core)
                slot = from_y // quarter
                value = block[pl.ds(row, strip)].astype(F32)
                moved = pltpu.roll(value, (slot - flip_core) * block_o + half, 1)
                keep = (lane >= slot * block_o) & (lane < (slot + 1) * block_o)
                pieces[flip_core, flip] = (jnp.where(keep, moved, 0.0), from_y % quarter)
        if quarter == 1:
            total = sum(p for p, _ in list(pieces.values())[1:]) + list(pieces.values())[0][0]
            totals = [(0, total)]
        else:
            totals = []
            for n in range(quarter):
                total = jnp.zeros((strip, chans), F32)
                for piece, place in pieces.values():
                    total = total + jnp.where(place == n, piece, 0.0)
                totals.append((n, total))
        for out, parity in zip(outs, (1, 0)):

            @pl.when((hi + from_lo) % 2 == parity)
            def _(out=out):
                for n, total in totals:
                    out[n * strip : (n + 1) * strip] = total.astype(BF16)


def unpack_body(dims, *refs):
    _, parts_y, wx, wy, depth, chans = dims
    _, lo, chip, core = spot()
    chips, half, block_o = parts_y // 2, chans // 2, chans // parts_y
    blocks, cot_ref = refs[: 4 * chips], refs[4 * chips]
    acts, wide, pad, cots = refs[4 * chips + 1 :]
    rows = wx * wy * depth
    total_y, strip = wy * parts_y, wy * depth
    lane = lax.broadcasted_iota(jnp.int32, (1, chans), 1)
    blank = jnp.zeros((depth, chans), BF16)
    for x in range(2 * wx):
        for slot in range(3):
            cots[slot, x, 0] = blank
            cots[slot, x, total_y + 1] = blank
    facing = (1 - lo) * (wx + 1)
    toward, away = (1 - core) * (wy + 1), core * (wy + 1)
    swapped = blocks[2 * chips :]
    pad[1 : wx + 1, 1 : wy + 1] = cot_ref[...]
    near_row = pl.multiple_of(rows + lo * (wx - 1) * depth, depth)
    pad[facing, toward] = swapped[chips][pl.ds(near_row, depth)]
    pad[facing, away] = blank
    for x in range(wx):
        pad[x + 1, toward] = swapped[0][rows + x * depth : rows + (x + 1) * depth]
        pad[x + 1, away] = blank
    for flip in near_flips(chips):

        @pl.when((chip ^ flip) == chip + 2 * core - 1)
        def _(flip=flip):
            pad[facing, away] = swapped[chips + flip][pl.ds(near_row, depth)]
            for x in range(wx):
                pad[x + 1, away] = swapped[flip][rows + x * depth : rows + (x + 1) * depth]

    place = 0
    for flip_core in range(2):
        for flip_lo in range(2):
            for flip in range(chips):
                block = blocks[place]
                place += 1
                first_x = (lo ^ flip_lo) * wx
                first_y = (2 * (chip ^ flip) + (core ^ flip_core)) * wy
                for x in range(wx):
                    part = block[x * strip : (x + 1) * strip]
                    acts[first_x + x, pl.ds(first_y, wy)] = part.reshape(wy, depth, chans)
                    value = part.astype(F32)
                    for slot in range(3):
                        shift = (slot - flip_core) * block_o - half
                        cots[slot, first_x + x, pl.ds(first_y + 1, wy)] = in_lanes(
                            value, shift, slot, block_o, lane
                        ).reshape(wy, depth, chans)

    def merge(y, carry):
        for x in range(2 * wx):
            wide[x + 1, y] = cots[0, x, y + 2] + cots[1, x, y + 1] + cots[2, x, y]
        wide[0, y] = blank
        wide[2 * wx + 1, y] = blank
        return carry

    lax.fori_loop(0, total_y, merge, 0, unroll=4)


def main_body(dims, acts, wide, sums, low, high):
    _, parts_y, wx, wy, depth, chans = dims
    half, total_y = chans // 2, wy * parts_y
    step = min(total_y, 16)
    z = lax.broadcasted_iota(jnp.int32, (depth, 1), 0)
    sums[...] = jnp.zeros_like(sums)
    for x in range(2 * wx):

        def chunk(n, carry, x=x):
            planes = pl.ds(n * step, step)
            middle = acts[x, planes][:, :, :half].astype(F32)
            below = jnp.where(z > 0, pltpu.roll(middle, 1, 1), 0.0)
            above = jnp.where(z < depth - 1, pltpu.roll(middle, depth - 1, 1), 0.0)
            left = jnp.concatenate([below, middle, above], axis=2).astype(BF16)
            left = left.reshape(step * depth, 3 * half)
            if x == 0:
                low[pl.ds(pl.multiple_of(n * step * depth, step * depth), step * depth)] = left
            if x == 2 * wx - 1:
                high[pl.ds(pl.multiple_of(n * step * depth, step * depth), step * depth)] = left
            right = jnp.concatenate(
                [wide[x + 2 - jx, planes].reshape(step * depth, chans) for jx in range(3)], axis=1
            )
            sums[...] += lax.dot_general(
                left, right, (((0,), (0,)), ((), ())), preferred_element_type=F32
            )
            return carry

        if total_y == step:
            chunk(0, 0)
        else:
            lax.fori_loop(0, total_y // step, chunk, 0)


def ends_body(dims, main_ref, low, high, even, odd, *refs):
    parts_x, parts_y, _, wy, depth, chans = dims
    hi, _, _, _ = spot()
    his = parts_x // 2
    block_i, half, block_o = chans // parts_x, chans // 2, chans // parts_y
    outs, (cots, sums) = refs[:his], refs[his:]
    total_y = wy * parts_y
    part_y = total_y // 4
    size = part_y * depth
    lane = lax.broadcasted_iota(jnp.int32, (1, chans), 1)
    blank = jnp.zeros((depth, chans), BF16)
    for end in range(2):
        for slot in range(3):
            cots[end, slot, 0] = blank
            cots[end, slot, total_y + 1] = blank
    for ref, end in ((even, 1 - hi % 2), (odd, hi % 2)):
        value = ref[:size].astype(F32)
        for slot in range(3):
            for part in range(4):
                cots[end, slot, 1 + part * part_y : 1 + (part + 1) * part_y] = in_lanes(
                    value, (slot - part) * block_o, slot, block_o, lane
                ).reshape(part_y, depth, chans)
    sums[...] = main_ref[...]
    for end, left, jx in ((0, low, 2), (1, high, 0)):
        right = cots[end, 0, 2 : total_y + 2] + cots[end, 1, 1 : total_y + 1]
        right = right + cots[end, 2, 0:total_y]
        sums[:, jx * chans : (jx + 1) * chans] += lax.dot_general(
            left[...],
            right.reshape(total_y * depth, chans),
            (((0,), (0,)), ((), ())),
            preferred_element_type=F32,
        )
    free = 3 * block_o
    for flip, out in enumerate(outs):
        start = pl.multiple_of((hi ^ flip) * block_i, block_i)

        def group(jx, jz):
            return sums[pl.ds(jz * half + start, block_i), jx * chans : (jx + 1) * chans]

        last = jnp.zeros((block_i, chans), F32)
        for jz in range(3):
            spare = group(2, jz)
            for jx in range(2):
                moved = pltpu.roll(spare, free - jx * block_o, 1)
                piece = jnp.where(lane < free, group(jx, jz), moved)
                out[(3 * jx + jz) * block_i : (3 * jx + jz + 1) * block_i] = piece.astype(out.dtype)
            moved = pltpu.roll(spare, ((jz - 2) * block_o) % chans, 1)
            keep = (lane >= jz * block_o) & (lane < (jz + 1) * block_o)
            last = jnp.where(keep, moved, last)
        out[6 * block_i :] = last.astype(out.dtype)


def back_body(dims, inputs_ref, pad_ref, outer_ref, inner_ref, even, odd, kernel_ref, out_ref, pad):
    _, parts_y, wx, wy, depth, chans = dims
    hi, lo, _, core = spot()
    rows = wx * wy * depth
    pad[...] = pad_ref[...]
    pad[(1 - lo) * (wx + 1), 1 : wy + 1] = inner_ref[...].reshape(wy, depth, chans)
    pad[lo * (wx + 1), 1 : wy + 1] = outer_ref[...].reshape(wy, depth, chans)
    toward, away = (1 - core) * (wy + 1), core * (wy + 1)
    size = wy * parts_y // 4 * depth
    for ref, parity in ((even, 1), (odd, 0)):

        @pl.when((hi + lo) % 2 == parity)
        def _(ref=ref):
            pad[lo * (wx + 1), toward] = ref[size : size + depth]
            pad[lo * (wx + 1), away] = ref[size + depth :]

    left, right = [], []
    for jx in range(3):
        for jy in range(3):
            first = jx * 9 + jy * 3
            piece = pad[2 - jx : 2 - jx + wx, 2 - jy : 2 - jy + wy]
            left.append(piece.reshape(rows, chans))
            right.append(kernel_ref[first : first + 3].reshape(3 * chans, chans))
    product = lax.dot_general(
        jnp.concatenate(left, axis=1),
        jnp.concatenate(right, axis=1),
        (((1,), (1,)), ((), ())),
        preferred_element_type=F32,
    ).reshape(wx * wy, depth, 3 * chans)
    z = lax.broadcasted_iota(jnp.int32, (depth, 1), 0)
    low = product[:, :, :chans]
    high = product[:, :, 2 * chans :]
    back = product[:, :, chans : 2 * chans]
    back += jnp.where(z < depth - 1, pltpu.roll(low, depth - 1, 1), 0.0)
    back += jnp.where(z > 0, pltpu.roll(high, 1, 1), 0.0)
    values = inputs_ref[...].astype(F32).reshape(wx * wy, depth, chans)
    cdf = gelu_parts(values)
    slope = cdf + values * jnp.exp(-0.5 * values * values) / math.sqrt(2.0 * math.pi)
    out_ref[...] = (slope * back).astype(BF16).reshape(wx, wy, depth, chans)


def final_body(dims, voxels, *refs):
    parts_x, parts_y, _, _, _, chans = dims
    block_i, block_o = chans // parts_x, chans // parts_y
    out = refs[-1]
    total = refs[0][...]
    for ref in refs[1:-1]:
        total = total + ref[...].astype(F32)
    total = total * (1.0 / math.sqrt(voxels))
    for jx in range(3):
        for jy in range(3):
            for jz in range(3):
                if jx < 2:
                    row, column = 3 * jx + jz, jy
                elif jy < 2:
                    row, column = 3 * jy + jz, 3
                else:
                    row, column = 6, jz
                out[9 * jx + 3 * jy + jz] = total[
                    row * block_i : (row + 1) * block_i, column * block_o : (column + 1) * block_o
                ]


def local(inputs, cotangent, kernel):
    wx, wy, depth, chans = inputs.shape
    parts_x, parts_y = lax.axis_size("gx"), lax.axis_size("gy")
    size = parts_x * parts_y
    his, chips = parts_x // 2, parts_y // 2
    dims = (parts_x, parts_y, wx, wy, depth, chans)
    rows = wx * wy * depth
    block_i, half = chans // parts_x, chans // 2
    total_y, total_x = wy * parts_y, 2 * wx
    face = (wy * depth, chans)
    near = [0, *near_flips(chips)]
    extras = [rows + wx * depth * (n % chips in near) for n in range(2 * chips)]

    count = 2 * chips
    *packed, outer, inner = call(
        functools.partial(pack_body, dims),
        [((n, chans), BF16) for n in extras] + [(face, BF16)] * 2,
        (inputs, cotangent),
        scratch=(
            pltpu.VMEM(inputs.shape, BF16),
            pltpu.VMEM(inputs.shape, BF16),
            pltpu.SemaphoreType.DMA((2,)),
        ),
        fetch=True,
        flops=2 * count * rows * 2 * chans * chans,
        moved=2 * (count + 3) * rows * chans,
    )
    masks = [a * parts_y + 2 * g for a in range(2) for g in range(chips)]
    same = [packed[0]] + [swap(packed[n], size, masks[n]) for n in range(1, count)]
    other = [swap(same[n], size, 1) for n in range(count)]
    outer = move(outer, pairs_along(parts_x, parts_y, size, True))
    inner = move(inner, pairs_along(parts_x, parts_y, size, False))

    end_even, end_odd = call(
        functools.partial(edges_body, dims),
        [(((total_y // 4 + 2) * depth, chans), BF16)] * 2,
        (*same, *other),
    )
    acts, wide, pad = call(
        functools.partial(unpack_body, dims),
        [
            ((total_x, total_y, depth, chans), BF16),
            ((total_x + 2, total_y, depth, chans), BF16),
            ((wx + 2, wy + 2, depth, chans), BF16),
        ],
        (*same, *other, cotangent),
        scratch=(pltpu.VMEM((3, total_x, total_y + 2, depth, chans), BF16),),
        moved=4 * count * rows * chans,
    )
    end_even = move(end_even, pairs_along(his, 2 * parts_y, size, False))
    end_odd = move(end_odd, pairs_along(his, 2 * parts_y, size, True))
    sums, low, high = call(
        functools.partial(main_body, dims),
        [((3 * half, 3 * chans), F32), ((total_y * depth, 3 * half), BF16), ((total_y * depth, 3 * half), BF16)],
        (acts, wide),
        flops=2 * total_x * total_y * depth * 9 * half * chans,
        moved=4 * count * rows * chans,
    )
    raw = call(
        functools.partial(ends_body, dims),
        [((7 * block_i, chans), BF16 if m else F32) for m in range(his)],
        (sums, low, high, end_even, end_odd),
        scratch=(
            pltpu.VMEM((2, 3, total_y + 2, depth, chans), BF16),
            pltpu.VMEM((3 * half, 3 * chans), F32),
        ),
        flops=4 * total_y * depth * 3 * half * chans,
        moved=4 * total_y * depth * chans,
    )
    terms = [raw[0]] + [swap(raw[m], size, m * 2 * parts_y) for m in range(1, his)]
    (input_grad,) = call(
        functools.partial(back_body, dims),
        [((wx, wy, depth, chans), BF16)],
        (inputs, pad, outer, inner, end_even, end_odd, kernel),
        scratch=(pltpu.VMEM((wx + 2, wy + 2, depth, chans), BF16),),
        flops=2 * rows * 27 * chans * chans,
        moved=2 * 27 * chans * chans,
    )
    voxels = wx * parts_x * wy * parts_y * depth
    (kernel_grad,) = call(
        functools.partial(final_body, dims, voxels),
        [((27, block_i, chans // parts_y), F32)],
        terms,
        moved=4 * his * 7 * block_i * chans,
        last=True,
    )
    return (input_grad, kernel_grad)


def solution(mesh):
    return jax.shard_map(
        local,
        mesh=mesh,
        in_specs=(P("gx", "gy", None, None), P("gx", "gy", None, None), P()),
        out_specs=(P("gx", "gy", None, None), P(None, "gx", "gy")),
        check_vma=False,
    )
```

```python
import functools
import math

import jax
import jax.numpy as jnp
from jax import lax
from jax.experimental import pallas as pl
from jax.experimental.pallas import tpu as pltpu
from jax.sharding import PartitionSpec as P


AXES = ("gx", "gy")
BF16 = jnp.bfloat16
F32 = jnp.float32


def near_flips(chips):
    return [(1 << k) - 1 for k in range(1, chips.bit_length())]


def spot():
    at_x, at_y = lax.axis_index("gx"), lax.axis_index("gy")
    return at_x // 2, at_x % 2, at_y // 2, at_y % 2


def move(array, pairs):
    return lax.ppermute(array, AXES, pairs)


def swap(array, size, mask):
    return move(array, [(i, i ^ mask) for i in range(size)])


def pairs_along(count, stride, size, odd):
    found = []
    for i in range(size):
        at = (i // stride) % count
        to = at ^ 1 if not odd else (at - 1 if at % 2 == 0 else at + 1)
        found.append((i, i + (to - at) * stride if 0 <= to < count else i ^ 1))
    return found


def call(body, outs, args, scratch=(), flops=0, moved=0, fetch=False, last=False):
    vmem = pl.BlockSpec(memory_space=pltpu.VMEM)
    run = pl.pallas_call(
        body,
        out_shape=tuple((jax.ShapeDtypeStruct if last else pltpu.VMEM)(s, d) for s, d in outs),
        in_specs=[pl.BlockSpec(memory_space=pltpu.HBM) if fetch else vmem] * len(args),
        out_specs=tuple(vmem for _ in outs),
        scratch_shapes=list(scratch),
        compiler_params=pltpu.CompilerParams(vmem_limit_bytes=32 << 20),
        cost_estimate=pl.CostEstimate(flops=flops, bytes_accessed=moved, transcendentals=0),
    )
    space = pltpu.HBM if fetch else pltpu.VMEM
    args = [pltpu.with_memory_space_constraint(a, space) for a in args]
    return run(*args)


def gelu_parts(values):
    cdf = 0.5 * (1.0 + lax.erf(values / math.sqrt(2.0)))
    return cdf


def pack_body(dims, inputs_hbm, cot_hbm, *refs):
    parts_x, parts_y, wx, wy, depth, chans = dims
    _, lo, chip, core = spot()
    chips = parts_y // 2
    block_i, half = chans // parts_x, chans // 2
    block_o = chans // parts_y
    rows = wx * wy * depth
    *outs, inputs_ref, cot_ref, arrived = refs
    copies = [
        pltpu.make_async_copy(inputs_hbm, inputs_ref, arrived.at[0]),
        pltpu.make_async_copy(cot_hbm, cot_ref, arrived.at[1]),
    ]
    for copy in copies:
        copy.start()
    for copy in copies:
        copy.wait()
    outs[-2][...] = cot_ref[lo * (wx - 1)].reshape(wy * depth, chans)
    outs[-1][...] = cot_ref[(1 - lo) * (wx - 1)].reshape(wy * depth, chans)
    for flip in [0, *near_flips(chips)]:
        column = (core if flip else 1 - core) * (wy - 1)
        for x in range(wx):
            plane = cot_ref[x, column]
            outs[flip][rows + x * depth : rows + (x + 1) * depth] = plane
            outs[chips + flip][rows + x * depth : rows + (x + 1) * depth] = plane
    values = inputs_ref[...].reshape(rows, chans).astype(F32)
    act = (values * gelu_parts(values)).astype(BF16)
    both = jnp.concatenate([act, cot_ref[...].reshape(rows, chans)], axis=1)
    lane = lax.broadcasted_iota(jnp.int32, (1, chans), 1)
    at = lax.broadcasted_iota(jnp.int32, (2 * chans, chans), 0)
    group = jnp.right_shift(lane, block_i.bit_length() - 1)
    column = lane - half
    side = jnp.right_shift(column, block_o.bit_length() - 1) ^ core
    for flip_lo in range(2):
        for flip in range(chips):
            to_lo, to_chip = lo ^ flip_lo, chip ^ flip
            from_act = (2 * group + to_lo) * block_i + (lane & (block_i - 1))
            from_cot = (2 * to_chip + side) * block_o + (column & (block_o - 1))
            from_cot = jnp.where(column < 2 * block_o, chans + from_cot, -1)
            chosen = (at == jnp.where(lane < half, from_act, from_cot)).astype(F32).astype(BF16)
            out = outs[flip_lo * chips + flip]
            out[:rows] = jnp.dot(both, chosen, preferred_element_type=F32).astype(BF16)


def in_lanes(value, shift, slot, width, lane):
    chans = value.shape[1]
    moved = pltpu.roll(value, shift % chans, 1) if shift % chans else value
    keep = (lane >= slot * width) & (lane < (slot + 1) * width)
    return jnp.where(keep, moved, 0.0).astype(BF16)


def edges_body(dims, *refs):
    _, parts_y, wx, wy, depth, chans = dims
    hi, lo, chip, core = spot()
    chips, half, block_o = parts_y // 2, chans // 2, chans // parts_y
    blocks, outs = refs[: 4 * chips], refs[4 * chips :]
    swapped = blocks[2 * chips :]
    strip, quarter = wy * depth, parts_y // 4
    rows, size = wx * strip, quarter * strip
    lane = lax.broadcasted_iota(jnp.int32, (1, chans), 1)
    far_row = pl.multiple_of(rows + (1 - lo) * (wx - 1) * depth, depth)
    for out in outs:
        out[size : size + depth] = swapped[chips][pl.ds(far_row, depth)]
        out[size + depth :] = jnp.zeros((depth, chans), BF16)
    for flip in near_flips(chips):

        @pl.when((chip ^ flip) == chip + 2 * core - 1)
        def _(flip=flip):
            for out in outs:
                out[size + depth :] = swapped[chips + flip][pl.ds(far_row, depth)]

    for flip_lo in range(2):
        from_lo = lo ^ flip_lo
        row = pl.multiple_of(from_lo * (wx - 1) * strip, strip)
        pieces = {}
        for flip_core in range(2):
            for flip in range(chips):
                block = blocks[(2 * flip_core + flip_lo) * chips + flip]
                from_y = 2 * (chip ^ flip) + (core ^ flip_core)
                slot = from_y // quarter
                value = block[pl.ds(row, strip)].astype(F32)
                moved = pltpu.roll(value, (slot - flip_core) * block_o + half, 1)
                keep = (lane >= slot * block_o) & (lane < (slot + 1) * block_o)
                pieces[flip_core, flip] = (jnp.where(keep, moved, 0.0), from_y % quarter)
        if quarter == 1:
            total = sum(p for p, _ in list(pieces.values())[1:]) + list(pieces.values())[0][0]
            totals = [(0, total)]
        else:
            totals = []
            for n in range(quarter):
                total = jnp.zeros((strip, chans), F32)
                for piece, place in pieces.values():
                    total = total + jnp.where(place == n, piece, 0.0)
                totals.append((n, total))
        for out, parity in zip(outs, (1, 0)):

            @pl.when((hi + from_lo) % 2 == parity)
            def _(out=out):
                for n, total in totals:
                    out[n * strip : (n + 1) * strip] = total.astype(BF16)


def unpack_body(dims, *refs):
    _, parts_y, wx, wy, depth, chans = dims
    _, lo, chip, core = spot()
    chips, half, block_o = parts_y // 2, chans // 2, chans // parts_y
    blocks, cot_ref = refs[: 4 * chips], refs[4 * chips]
    acts, wide, pad, cots = refs[4 * chips + 1 :]
    rows = wx * wy * depth
    total_y, strip = wy * parts_y, wy * depth
    lane = lax.broadcasted_iota(jnp.int32, (1, chans), 1)
    blank = jnp.zeros((depth, chans), BF16)
    for x in range(2 * wx):
        for slot in range(3):
            cots[slot, x, 0] = blank
            cots[slot, x, total_y + 1] = blank
    facing = (1 - lo) * (wx + 1)
    toward, away = (1 - core) * (wy + 1), core * (wy + 1)
    swapped = blocks[2 * chips :]
    pad[1 : wx + 1, 1 : wy + 1] = cot_ref[...]
    near_row = pl.multiple_of(rows + lo * (wx - 1) * depth, depth)
    pad[facing, toward] = swapped[chips][pl.ds(near_row, depth)]
    pad[facing, away] = blank
    for x in range(wx):
        pad[x + 1, toward] = swapped[0][rows + x * depth : rows + (x + 1) * depth]
        pad[x + 1, away] = blank
    for flip in near_flips(chips):

        @pl.when((chip ^ flip) == chip + 2 * core - 1)
        def _(flip=flip):
            pad[facing, away] = swapped[chips + flip][pl.ds(near_row, depth)]
            for x in range(wx):
                pad[x + 1, away] = swapped[flip][rows + x * depth : rows + (x + 1) * depth]

    place = 0
    for flip_core in range(2):
        for flip_lo in range(2):
            for flip in range(chips):
                block = blocks[place]
                place += 1
                first_x = (lo ^ flip_lo) * wx
                first_y = (2 * (chip ^ flip) + (core ^ flip_core)) * wy
                for x in range(wx):
                    part = block[x * strip : (x + 1) * strip]
                    acts[first_x + x, pl.ds(first_y, wy)] = part.reshape(wy, depth, chans)
                    value = part.astype(F32)
                    for slot in range(3):
                        shift = (slot - flip_core) * block_o - half
                        cots[slot, first_x + x, pl.ds(first_y + 1, wy)] = in_lanes(
                            value, shift, slot, block_o, lane
                        ).reshape(wy, depth, chans)

    def merge(y, carry):
        for x in range(2 * wx):
            wide[x + 1, y] = cots[0, x, y + 2] + cots[1, x, y + 1] + cots[2, x, y]
        wide[0, y] = blank
        wide[2 * wx + 1, y] = blank
        return carry

    lax.fori_loop(0, total_y, merge, 0, unroll=4)


def main_body(dims, acts, wide, sums, low, high):
    _, parts_y, wx, wy, depth, chans = dims
    half, total_y = chans // 2, wy * parts_y
    step = min(total_y, 16)
    z = lax.broadcasted_iota(jnp.int32, (depth, 1), 0)
    sums[...] = jnp.zeros_like(sums)
    for x in range(2 * wx):

        def chunk(n, carry, x=x):
            planes = pl.ds(n * step, step)
            middle = acts[x, planes][:, :, :half].astype(F32)
            below = jnp.where(z > 0, pltpu.roll(middle, 1, 1), 0.0)
            above = jnp.where(z < depth - 1, pltpu.roll(middle, depth - 1, 1), 0.0)
            left = jnp.concatenate([below, middle, above], axis=2).astype(BF16)
            left = left.reshape(step * depth, 3 * half)
            if x == 0:
                low[pl.ds(pl.multiple_of(n * step * depth, step * depth), step * depth)] = left
            if x == 2 * wx - 1:
                high[pl.ds(pl.multiple_of(n * step * depth, step * depth), step * depth)] = left
            right = jnp.concatenate(
                [wide[x + 2 - jx, planes].reshape(step * depth, chans) for jx in range(3)], axis=1
            )
            sums[...] += lax.dot_general(
                left, right, (((0,), (0,)), ((), ())), preferred_element_type=F32
            )
            return carry

        if total_y == step:
            chunk(0, 0)
        else:
            lax.fori_loop(0, total_y // step, chunk, 0)


def ends_body(dims, main_ref, low, high, even, odd, *refs):
    parts_x, parts_y, _, wy, depth, chans = dims
    hi, _, _, _ = spot()
    his = parts_x // 2
    block_i, half, block_o = chans // parts_x, chans // 2, chans // parts_y
    outs, (cots, sums) = refs[:his], refs[his:]
    total_y = wy * parts_y
    part_y = total_y // 4
    size = part_y * depth
    lane = lax.broadcasted_iota(jnp.int32, (1, chans), 1)
    blank = jnp.zeros((depth, chans), BF16)
    for end in range(2):
        for slot in range(3):
            cots[end, slot, 0] = blank
            cots[end, slot, total_y + 1] = blank
    for ref, end in ((even, 1 - hi % 2), (odd, hi % 2)):
        inside = jnp.where(end == 1, hi < his - 1, hi > 0)
        value = jnp.where(inside, ref[:size].astype(F32), 0.0)
        for slot in range(3):
            for part in range(4):
                cots[end, slot, 1 + part * part_y : 1 + (part + 1) * part_y] = in_lanes(
                    value, (slot - part) * block_o, slot, block_o, lane
                ).reshape(part_y, depth, chans)
    sums[...] = main_ref[...]
    for end, left, jx in ((0, low, 2), (1, high, 0)):
        right = cots[end, 0, 2 : total_y + 2] + cots[end, 1, 1 : total_y + 1]
        right = right + cots[end, 2, 0:total_y]
        sums[:, jx * chans : (jx + 1) * chans] += lax.dot_general(
            left[...],
            right.reshape(total_y * depth, chans),
            (((0,), (0,)), ((), ())),
            preferred_element_type=F32,
        )
    free = 3 * block_o
    for flip, out in enumerate(outs):
        start = pl.multiple_of((hi ^ flip) * block_i, block_i)

        def group(jx, jz):
            return sums[pl.ds(jz * half + start, block_i), jx * chans : (jx + 1) * chans]

        last = jnp.zeros((block_i, chans), F32)
        for jz in range(3):
            spare = group(2, jz)
            for jx in range(2):
                moved = pltpu.roll(spare, free - jx * block_o, 1)
                piece = jnp.where(lane < free, group(jx, jz), moved)
                out[(3 * jx + jz) * block_i : (3 * jx + jz + 1) * block_i] = piece.astype(out.dtype)
            moved = pltpu.roll(spare, ((jz - 2) * block_o) % chans, 1)
            keep = (lane >= jz * block_o) & (lane < (jz + 1) * block_o)
            last = jnp.where(keep, moved, last)
        out[6 * block_i :] = last.astype(out.dtype)


def back_body(dims, inputs_ref, pad_ref, outer_ref, inner_ref, even, odd, kernel_ref, out_ref, pad):
    parts_x, parts_y, wx, wy, depth, chans = dims
    hi, lo, _, core = spot()
    rows = wx * wy * depth
    pad[...] = pad_ref[...]
    pad[(1 - lo) * (wx + 1), 1 : wy + 1] = inner_ref[...].reshape(wy, depth, chans)
    pad[lo * (wx + 1), 1 : wy + 1] = outer_ref[...].reshape(wy, depth, chans)
    toward, away = (1 - core) * (wy + 1), core * (wy + 1)
    size = wy * parts_y // 4 * depth
    for ref, parity in ((even, 1), (odd, 0)):

        @pl.when((hi + lo) % 2 == parity)
        def _(ref=ref):
            pad[lo * (wx + 1), toward] = ref[size : size + depth]
            pad[lo * (wx + 1), away] = ref[size + depth :]

    @pl.when(jnp.where(lo == 0, hi == 0, hi == parts_x // 2 - 1))
    def _():
        pad[lo * (wx + 1)] = jnp.zeros((wy + 2, depth, chans), BF16)

    left, right = [], []
    for jx in range(3):
        for jy in range(3):
            first = jx * 9 + jy * 3
            piece = pad[2 - jx : 2 - jx + wx, 2 - jy : 2 - jy + wy]
            left.append(piece.reshape(rows, chans))
            right.append(kernel_ref[first : first + 3].reshape(3 * chans, chans))
    product = lax.dot_general(
        jnp.concatenate(left, axis=1),
        jnp.concatenate(right, axis=1),
        (((1,), (1,)), ((), ())),
        preferred_element_type=F32,
    ).reshape(wx * wy, depth, 3 * chans)
    z = lax.broadcasted_iota(jnp.int32, (depth, 1), 0)
    low = product[:, :, :chans]
    high = product[:, :, 2 * chans :]
    back = product[:, :, chans : 2 * chans]
    back += jnp.where(z < depth - 1, pltpu.roll(low, depth - 1, 1), 0.0)
    back += jnp.where(z > 0, pltpu.roll(high, 1, 1), 0.0)
    values = inputs_ref[...].astype(F32).reshape(wx * wy, depth, chans)
    cdf = gelu_parts(values)
    slope = cdf + values * jnp.exp(-0.5 * values * values) / math.sqrt(2.0 * math.pi)
    out_ref[...] = (slope * back).astype(BF16).reshape(wx, wy, depth, chans)


def final_body(dims, voxels, *refs):
    parts_x, parts_y, _, _, _, chans = dims
    block_i, block_o = chans // parts_x, chans // parts_y
    out = refs[-1]
    total = refs[0][...]
    for ref in refs[1:-1]:
        total = total + ref[...].astype(F32)
    total = total * (1.0 / math.sqrt(voxels))
    for jx in range(3):
        for jy in range(3):
            for jz in range(3):
                if jx < 2:
                    row, column = 3 * jx + jz, jy
                elif jy < 2:
                    row, column = 3 * jy + jz, 3
                else:
                    row, column = 6, jz
                out[9 * jx + 3 * jy + jz] = total[
                    row * block_i : (row + 1) * block_i, column * block_o : (column + 1) * block_o
                ]


def local(inputs, cotangent, kernel):
    wx, wy, depth, chans = inputs.shape
    parts_x, parts_y = lax.axis_size("gx"), lax.axis_size("gy")
    size = parts_x * parts_y
    his, chips = parts_x // 2, parts_y // 2
    dims = (parts_x, parts_y, wx, wy, depth, chans)
    rows = wx * wy * depth
    block_i, half = chans // parts_x, chans // 2
    total_y, total_x = wy * parts_y, 2 * wx
    face = (wy * depth, chans)
    near = [0, *near_flips(chips)]
    extras = [rows + wx * depth * (n % chips in near) for n in range(2 * chips)]

    count = 2 * chips
    *packed, outer, inner = call(
        functools.partial(pack_body, dims),
        [((n, chans), BF16) for n in extras] + [(face, BF16)] * 2,
        (inputs, cotangent),
        scratch=(
            pltpu.VMEM(inputs.shape, BF16),
            pltpu.VMEM(inputs.shape, BF16),
            pltpu.SemaphoreType.DMA((2,)),
        ),
        fetch=True,
        flops=2 * count * rows * 2 * chans * chans,
        moved=2 * (count + 3) * rows * chans,
    )
    masks = [a * parts_y + 2 * g for a in range(2) for g in range(chips)]
    same = [packed[0]] + [swap(packed[n], size, masks[n]) for n in range(1, count)]
    other = [swap(same[n], size, 1) for n in range(count)]
    outer = move(outer, pairs_along(parts_x, parts_y, size, True))
    inner = move(inner, pairs_along(parts_x, parts_y, size, False))

    end_even, end_odd = call(
        functools.partial(edges_body, dims),
        [(((total_y // 4 + 2) * depth, chans), BF16)] * 2,
        (*same, *other),
    )
    acts, wide, pad = call(
        functools.partial(unpack_body, dims),
        [
            ((total_x, total_y, depth, chans), BF16),
            ((total_x + 2, total_y, depth, chans), BF16),
            ((wx + 2, wy + 2, depth, chans), BF16),
        ],
        (*same, *other, cotangent),
        scratch=(pltpu.VMEM((3, total_x, total_y + 2, depth, chans), BF16),),
        moved=4 * count * rows * chans,
    )
    end_even = move(end_even, pairs_along(his, 2 * parts_y, size, False))
    end_odd = move(end_odd, pairs_along(his, 2 * parts_y, size, True))
    sums, low, high = call(
        functools.partial(main_body, dims),
        [((3 * half, 3 * chans), F32), ((total_y * depth, 3 * half), BF16), ((total_y * depth, 3 * half), BF16)],
        (acts, wide),
        flops=2 * total_x * total_y * depth * 9 * half * chans,
        moved=4 * count * rows * chans,
    )
    raw = call(
        functools.partial(ends_body, dims),
        [((7 * block_i, chans), BF16 if m else F32) for m in range(his)],
        (sums, low, high, end_even, end_odd),
        scratch=(
            pltpu.VMEM((2, 3, total_y + 2, depth, chans), BF16),
            pltpu.VMEM((3 * half, 3 * chans), F32),
        ),
        flops=4 * total_y * depth * 3 * half * chans,
        moved=4 * total_y * depth * chans,
    )
    terms = [raw[0]] + [swap(raw[m], size, m * 2 * parts_y) for m in range(1, his)]
    (input_grad,) = call(
        functools.partial(back_body, dims),
        [((wx, wy, depth, chans), BF16)],
        (inputs, pad, outer, inner, end_even, end_odd, kernel),
        scratch=(pltpu.VMEM((wx + 2, wy + 2, depth, chans), BF16),),
        flops=2 * rows * 27 * chans * chans,
        moved=2 * 27 * chans * chans,
    )
    voxels = wx * parts_x * wy * parts_y * depth
    (kernel_grad,) = call(
        functools.partial(final_body, dims, voxels),
        [((27, block_i, chans // parts_y), F32)],
        terms,
        moved=4 * his * 7 * block_i * chans,
        last=True,
    )
    return (input_grad, kernel_grad)


def solution(mesh):
    return jax.shard_map(
        local,
        mesh=mesh,
        in_specs=(P("gx", "gy", None, None), P("gx", "gy", None, None), P()),
        out_specs=(P("gx", "gy", None, None), P(None, "gx", "gy")),
        check_vma=False,
    )
```
